32 devices in a mesh: groups: 2 (over y), expert: 4 (over x, core), tensor: 4 (over z).
Axes of the slice: x: 2, y: 2, z: 4, core: 2. Of those that a mesh axis runs over, the one named last changes fastest.
Arguments:
- tokens: bfloat16 [2048, 2048], P(('groups', 'expert')), parts along dimension 0, may hold values from -6 to 6
- route_ids: int32 [2048, 2], P(('groups', 'expert')), parts along dimension 0, may hold values from 0 to 3, all different within a row; in each aligned block of 256 rows (0 to 255, 256 to 511, ...) at most 256 rows name the same one
- route_weights: float32 [2048, 2], P(('groups', 'expert')), parts along dimension 0, may hold values from 0.2 to 1
- modulation: float32 [8, 6144], P(('groups', 'expert')), parts along dimension 0, may hold values from -5 to 5
- partner: int32 [4], replicated, may hold values from 0 to 3, as said below
- w_gate: bfloat16 [4, 2048, 4096], P('expert', None, 'tensor'), may hold values from -0.125 to 0.125
- w_up: bfloat16 [4, 2048, 4096], P('expert', None, 'tensor'), may hold values from -0.125 to 0.125
- w_down: bfloat16 [4, 4096, 2048], P('expert', 'tensor'), may hold values from -0.09375 to 0.09375
- spare_gate: bfloat16 [4, 2048, 4096], P('expert', None, 'tensor'), may hold values from -0.125 to 0.125
- spare_up: bfloat16 [4, 2048, 4096], P('expert', None, 'tensor'), may hold values from -0.125 to 0.125
- spare_down: bfloat16 [4, 4096, 2048], P('expert', 'tensor'), may hold values from -0.09375 to 0.09375
Outputs:
- layer_out: bfloat16 [2048, 2048], P(('groups', 'expert'), 'tensor'), parts along dimension 0
The draws below stay inside these ranges and needn't reach their ends.
There are 2 independent parts, one for each index of `groups`. The reference program is written for one: setup_inputs(seed, part) draws one part's arguments, and reference() takes and returns one part's arrays. A program takes and returns all parts, laid end to end along the dimension named above; an argument that names none is the same for every part. Nothing has to cross between parts.
Inputs may be any that keep to these rules, and one draw needn't show every extreme that they name: `route_ids`: the two ids of a token differ. Within the 256 tokens of one image no expert is named more than 2 * 128 times; in some image some expert is named exactly 2 * 128 times. partner is a permutation of the experts with partner[e] != e for every e.
All inputs are finite; a program needn't handle non-finite values.
Results may differ from the reference program's by a relative error of at most 0.014.
Values may be sent and summed in bfloat16 or wider, within the bound.
No kernel may reach another device: no remote copies, remote signals or barrier semaphores. Data moves between devices by JAX's collectives and lax.ppermute only.
A program may use at most 64 MiB of HBM per device.

```python
import math
import jax
import jax.numpy as jnp
import numpy as np
from jax import lax

D = 2048
FF = 4096
TOK_DEV = 256
EXPERTS = 4
IMAGES = 4
TOKENS = 1024
CAP = 128
N_TENSOR = 4


def draw_partner(key, part):
    order = jax.random.permutation(key, EXPERTS).astype(jnp.int32)
    following = jnp.roll(order, -1)
    return jnp.zeros((EXPERTS,), jnp.int32).at[order].set(following).astype(jnp.int32)


def shard_levels(rng, extent, shards, low, largest):
    level = 1.0
    for axis_at, shards_of in shards:
        heights = jax.random.uniform(jax.random.fold_in(jax.random.fold_in(rng, 6), axis_at), (shards_of,), jnp.float32, low / len(shards), largest / len(shards))
        level = level * jnp.repeat(jnp.exp(heights), extent[axis_at] // shards_of).reshape((-1,) + (1,) * (len(extent) - 1 - axis_at))
    return level


def deal_out(stream_key, own, number, rows, count, top, bound, lean):
    sequence = jax.random.permutation(stream_key, count)
    crowded, ordinary = portions_of(count, rows * top, bound, lean, True), portions_of(count, rows * top, bound, lean, False)
    places = jnp.arange(count)

    def named(lengths, offset_by):
        used = int((lengths > 0).sum())
        fixed = max(1, used // 4)
        shifted = fixed + (places - fixed + offset_by * (used - fixed)) % max(1, count - fixed)
        return jnp.zeros((count,), jnp.int32).at[sequence[jnp.where(places < fixed, places, shifted)]].set(jnp.asarray(lengths, jnp.int32))

    lengths = jnp.where(number % 4 == 0, named(crowded, number // 4), named(ordinary, number - number // 4 - 1))
    mixed = jax.random.permutation(jax.random.fold_in(own, 3), count)
    giver, taker = mixed[0:count // 2 * 2:2], mixed[1:count // 2 * 2:2]
    slack = jnp.minimum(lengths[giver] - 1, bound - lengths[taker]) // 2
    slack = jnp.where((giver == sequence[0]) | (taker == sequence[0]) | (lengths[taker] == 0), 0, jnp.maximum(slack, 0))
    shifted = jax.random.randint(jax.random.fold_in(own, 4), (count // 2,), 0, 1 << 20) % (slack + 1)
    lengths = lengths.at[giver].add(-shifted).at[taker].add(shifted)
    labels = jnp.searchsorted(jnp.cumsum(lengths), jnp.arange(rows * top), side="right").astype(jnp.int32)
    grid = labels.reshape(top, rows).T
    grid = grid[jax.random.permutation(jax.random.fold_in(own, 1), rows)]
    offset_by = jax.random.randint(jax.random.fold_in(own, 2), (rows, 1), 0, top)
    return jnp.take_along_axis(grid, (jnp.arange(top)[None, :] + offset_by) % top, axis=1)


def portions_of(number_of, total, most, lean, full):
    loads = [(1 << 20) // math.isqrt(rank ** lean) + 1 for rank in range(1, number_of + 1)]
    largest = most if full else min(most, max(-(-total // number_of), total * loads[0] // sum(loads)))
    least = 1 if total - largest >= number_of - 1 else 0
    given, spare = [largest] + [least] * (number_of - 1), total - largest - least * (number_of - 1)
    while spare > 0:
        candidates = [i for i in range(1, number_of) if given[i] < largest] or [i for i in range(1, number_of) if given[i] < most]
        whole, left = sum([loads[i] for i in candidates]), spare
        for i in candidates:
            more = min(most - given[i], max(1, left * loads[i] // whole), spare)
            given[i] = given[i] + more
            spare = spare - more
    return np.array(given)


def normal_values(stream_key, shape, scale, most, cuts=(), kind=jnp.bfloat16):
    gain = shard_levels(stream_key, shape, cuts, -0.22, 0.18) if cuts else 1.0
    values = jax.random.normal(stream_key, shape, jnp.float32) * scale * gain
    return jnp.minimum(jnp.maximum(values, -most), most).astype(kind)


def setup_inputs(seed: int = 0, part: int = 0) -> dict:
    key_of = jax.random.split(jax.random.key(seed), 12)
    part_splits = jax.random.split(jax.random.fold_in(key_of[11], part), 12)
    tokens = normal_values(part_splits[0], (TOKENS, D), 1.0, 6.0, ((0, 4),))
    route_ids_keys = jax.random.split(jax.random.fold_in(part_splits[1], 1), TOKENS // TOK_DEV)
    route_ids_turns = jax.random.permutation(jax.random.fold_in(part_splits[1], 3), TOKENS // TOK_DEV)
    route_ids = jax.vmap(lambda own, number: deal_out(jax.random.fold_in(part_splits[1], 2), own, number, TOK_DEV, EXPERTS, 2, 2 * CAP, 2))(route_ids_keys, route_ids_turns).reshape((TOKENS, 2))
    route_weights = jnp.clip(0.2 + 0.8 * jax.random.uniform(part_splits[2], (TOKENS, 2), jnp.float32) ** shard_levels(part_splits[2], (TOKENS, 2), ((0, 4),), -0.2, 0.2), 0.2, 1.0)
    modulation = normal_values(part_splits[3], (IMAGES, 3 * D), 1.0, 5.0, ((0, 4),), jnp.float32)
    partner = draw_partner(jax.random.fold_in(key_of[11], 71), part)
    w_gate = normal_values(key_of[5], (EXPERTS, D, FF), D ** -0.5, 0.125, ((0, 4), (2, 4)))
    w_up = normal_values(key_of[6], (EXPERTS, D, FF), D ** -0.5, 0.125, ((0, 4), (2, 4)))
    w_down = normal_values(key_of[7], (EXPERTS, FF, D), FF ** -0.5, 0.09375, ((0, 4), (1, 4)))
    spare_gate = normal_values(key_of[8], (EXPERTS, D, FF), D ** -0.5, 0.125, ((0, 4), (2, 4)))
    spare_up = normal_values(key_of[9], (EXPERTS, D, FF), D ** -0.5, 0.125, ((0, 4), (2, 4)))
    spare_down = normal_values(key_of[10], (EXPERTS, FF, D), FF ** -0.5, 0.09375, ((0, 4), (1, 4)))
    return dict(tokens=tokens, route_ids=route_ids, route_weights=route_weights, modulation=modulation, partner=partner, w_gate=w_gate, w_up=w_up, w_down=w_down, spare_gate=spare_gate, spare_up=spare_up, spare_down=spare_down)


def slot_targets(ids, partner):
    flat = ids.reshape(-1).astype(jnp.int32)
    onehot = (flat[:, None] == jnp.arange(EXPERTS, dtype=jnp.int32)[None, :]).astype(jnp.int32)
    ranks = lax.optimization_barrier(jnp.sum((jnp.cumsum(onehot, axis=0) - 1) * onehot, axis=1)).astype(jnp.int32)
    spare_of = lax.optimization_barrier(jnp.sum(onehot * partner[None, :].astype(jnp.int32), axis=1)).astype(jnp.int32)
    server = jnp.where(ranks >= CAP, spare_of, flat).astype(jnp.int32)
    return (server * (2 * CAP) + ranks).astype(jnp.int32)

def modulate(block, mod_row):
    values = block.astype(jnp.float32)
    mean = lax.optimization_barrier(jnp.mean(values, axis=1, keepdims=True))
    centred = values - mean
    var = lax.optimization_barrier(jnp.mean(centred * centred, axis=1, keepdims=True))
    normed = centred / jnp.sqrt(var + 1e-06)
    return (normed * (1.0 + mod_row[D:2 * D]) + mod_row[0:D]).astype(jnp.bfloat16)

def expert_apply(rows, gate_w, up_w, down_w):
    width = FF // N_TENSOR
    total = jnp.zeros((rows.shape[0], D), jnp.float32)
    for shard in range(N_TENSOR):
        lower = shard * width
        gate = jnp.dot(rows, gate_w[:, lower:lower + width], preferred_element_type=jnp.float32)
        upper = jnp.dot(rows, up_w[:, lower:lower + width], preferred_element_type=jnp.float32)
        hidden = (jax.nn.silu(gate) * upper).astype(jnp.bfloat16)
        piece = jnp.dot(hidden, down_w[lower:lower + width, :], preferred_element_type=jnp.float32).astype(jnp.bfloat16)
        piece = lax.optimization_barrier(piece)
        total = total + piece.astype(jnp.float32)
    return total

def device_apply(operands):
    block, gate_w, up_w, down_w, gate_s, up_s, down_s = operands
    home = expert_apply(block[:, 0].reshape(IMAGES * CAP, D), gate_w, up_w, down_w)
    spare = expert_apply(block[:, 1].reshape(IMAGES * CAP, D), gate_s, up_s, down_s)
    return jnp.stack((home.reshape(IMAGES, CAP, D), spare.reshape(IMAGES, CAP, D)), axis=1)

def reference(tokens, route_ids, route_weights, modulation, partner, w_gate, w_up, w_down, spare_gate, spare_up, spare_down):
    blocks = tokens.reshape(IMAGES, TOK_DEV, D)
    modded = jax.vmap(modulate)(blocks, modulation)
    targets = jax.vmap(slot_targets, in_axes=(0, None))(route_ids.reshape(IMAGES, TOK_DEV, 2), partner)

    def fill(rows, target):
        spread = jnp.repeat(rows, 2, axis=0)
        return jnp.zeros((EXPERTS * 2 * CAP, D), jnp.bfloat16).at[target].set(spread)
    sent = jax.vmap(fill)(modded, targets).reshape(IMAGES, EXPERTS, 2, CAP, D)
    arrived = jnp.transpose(sent, (1, 0, 2, 3, 4))
    outputs = lax.map(device_apply, (arrived, w_gate, w_up, w_down, spare_gate, spare_up, spare_down))
    outputs = jnp.transpose(outputs, (1, 0, 2, 3, 4)).reshape(IMAGES, EXPERTS * 2 * CAP, D)

    def finish(block, result, target, weights, mod_row):
        picked = result[target].reshape(TOK_DEV, 2, D)
        mixed = lax.optimization_barrier(jnp.sum(picked * weights[:, :, None], axis=1))
        return (block.astype(jnp.float32) + mod_row[2 * D:3 * D] * mixed).astype(jnp.bfloat16)
    final = jax.vmap(finish)(blocks, outputs, targets, route_weights.reshape(IMAGES, TOK_DEV, 2), modulation)
    return final.reshape(TOKENS, D)
```

```python
import functools

import jax
import jax.numpy as jnp
from jax import lax
from jax.experimental import pallas as pl
from jax.experimental.pallas import tpu as pltpu
from jax.sharding import PartitionSpec as P

LANES = 128
VMEM_LIMIT = 56 * 1024 * 1024
BF16 = jnp.bfloat16
F32 = jnp.float32


def prepare_kernel(experts, capacity, tok_ref, ids_ref, rw_ref, mod_ref, late_ref, early_ref, meta_ref):
    rows, width = tok_ref.shape
    values = tok_ref[...].astype(F32)
    mean = jnp.mean(values, axis=1, keepdims=True)
    centred = values - mean
    var = jnp.mean(centred * centred, axis=1, keepdims=True)
    inverse = 1.0 / jnp.sqrt(var + 1e-06)
    shift = mod_ref[:, 0:width]
    scale = mod_ref[:, width : 2 * width]
    modded = ((centred * inverse) * (1.0 + scale) + shift).astype(BF16)
    early_ref[...] = modded[:capacity]
    late_ref[...] = modded[capacity:]
    lane = lax.broadcasted_iota(jnp.int32, (rows, LANES), 1)
    quarter = lane // experts
    expert = lane - quarter * experts
    first = ids_ref[:, 0:1] == expert
    second = ids_ref[:, 1:2] == expert
    named = jnp.where(first | second, 1.0, 0.0).astype(BF16)
    row = lax.broadcasted_iota(jnp.int32, (rows, rows), 0)
    col = lax.broadcasted_iota(jnp.int32, (rows, rows), 1)
    below = jnp.where(col < row, 1.0, 0.0).astype(BF16)
    rank = jnp.dot(below, named, preferred_element_type=F32)
    weight = jnp.where(first, rw_ref[:, 0:1], 0.0) + jnp.where(second, rw_ref[:, 1:2], 0.0)
    high = weight.astype(BF16).astype(F32)
    part = jnp.where((quarter == 0) | (quarter == 2), high, weight - high)
    own = rank < float(capacity)
    wanted = ((quarter < 2) & own) | ((quarter >= 2) & (quarter < 4) & jnp.logical_not(own))
    meta_ref[...] = jnp.where(wanted, part, 0.0).astype(BF16)


def prepare(tokens, ids, weights, modulation, experts, capacity):
    rows, width = tokens.shape
    return pl.pallas_call(
        functools.partial(prepare_kernel, experts, capacity),
        out_shape=(
            jax.ShapeDtypeStruct((rows - capacity, width), BF16),
            jax.ShapeDtypeStruct((capacity, width), BF16),
            jax.ShapeDtypeStruct((rows, LANES), BF16),
        ),
        compiler_params=pltpu.CompilerParams(vmem_limit_bytes=24 * 1024 * 1024),
        cost_estimate=pl.CostEstimate(flops=12 * rows * width, bytes_accessed=4 * rows * width, transcendentals=0),
        name="prepare",
    )(tokens, ids, weights, modulation)


def ffn_kernel(experts, spans, spare_rows, blocks, shards, *refs):
    count = len(spans)
    partner_ref = refs[0]
    x_refs = refs[1 : 1 + count]
    meta_refs = refs[1 + count : 1 + 2 * count]
    rest = refs[1 + 2 * count :]
    home = rest[:3]
    spare = rest[3:6] if spare_rows else None
    rest = rest[6:] if spare_rows else rest[3:]
    out_refs = rest[:count]
    x_all, route, total = rest[count:]
    step = pl.program_id(0)
    steps = 2 * blocks if spare_rows else blocks
    width = x_all.shape[1]

    @pl.when(step == 0)
    def _():
        me = lax.axis_index("expert")
        source = jnp.int32(0)
        for e in range(experts):
            source = jnp.where(partner_ref[e] == me, e, source)
        start = 0
        for x_ref, meta_ref, (low, size) in zip(x_refs, meta_refs, spans):
            x_all[start : start + size, :] = x_ref[...]
            meta = meta_ref[low : low + size, :].astype(F32)
            lane = lax.broadcasted_iota(jnp.int32, (size, LANES), 1)
            mine = jnp.where((lane == me) | (lane == experts + me), meta, 0.0)
            route[0, start : start + size, :] = jnp.broadcast_to(
                jnp.sum(mine, axis=1, keepdims=True), (size, LANES)
            )
            theirs = jnp.where((lane == 2 * experts + source) | (lane == 3 * experts + source), meta, 0.0)
            route[1, start : start + size, :] = jnp.broadcast_to(
                jnp.sum(theirs, axis=1, keepdims=True), (size, LANES)
            )
            start += size

    def apply(which, height, weights):
        gate_w, up_w, down_w = weights
        values = x_all[:height, :]
        gate = jnp.dot(values, gate_w[0], preferred_element_type=F32)
        up = jnp.dot(values, up_w[0], preferred_element_type=F32)
        scaled = up * route[which, :height, 0:1]
        hidden = (gate / (1.0 + jnp.exp(-gate)) * scaled).astype(BF16)
        return jnp.dot(hidden, down_w[0], preferred_element_type=F32)

    height = x_all.shape[0]

    @pl.when(step == 0)
    def _():
        total[...] = apply(0, height, home)

    @pl.when((step > 0) & (step < blocks))
    def _():
        total[...] += apply(0, height, home)

    if spare_rows:

        @pl.when(step >= blocks)
        def _():
            total[:spare_rows, :] += apply(1, spare_rows, spare)

    @pl.when(step == steps - 1)
    def _():
        cols = width // shards
        start = 0
        for out_ref, (low, size) in zip(out_refs, spans):
            for shard in range(shards):
                out_ref[shard] = total[start : start + size, shard * cols : (shard + 1) * cols].astype(BF16)
            start += size


def ffn(name, xs, metas, spans, spare_rows, partner, home_set, spare_set, experts, shards, block=256):
    width = xs[0].shape[1]
    hidden = home_set[0].shape[2]
    block = min(block, hidden)
    blocks = hidden // block
    height = sum(size for _, size in spans)
    steps = 2 * blocks if spare_rows else blocks

    def weight_specs(at):
        return [
            pl.BlockSpec((1, width, block), lambda i: (0, 0, at(i))),
            pl.BlockSpec((1, width, block), lambda i: (0, 0, at(i))),
            pl.BlockSpec((1, block, width), lambda i: (0, at(i), 0)),
        ]

    whole = lambda a: pl.BlockSpec(a.shape, lambda i: (0,) * a.ndim)
    in_specs = [pl.BlockSpec(memory_space=pltpu.SMEM)] + [whole(a) for a in xs] + [whole(a) for a in metas]
    in_specs += weight_specs(lambda i: jnp.minimum(i, blocks - 1))
    operands = [partner, *xs, *metas, *home_set]
    if spare_rows:
        in_specs += weight_specs(lambda i: jnp.maximum(i - blocks, 0))
        operands += spare_set
    out_shape = [jax.ShapeDtypeStruct((shards, size, width // shards), BF16) for _, size in spans]
    work = height + spare_rows
    return pl.pallas_call(
        functools.partial(ffn_kernel, experts, spans, spare_rows, blocks, shards),
        out_shape=out_shape,
        grid=(steps,),
        in_specs=in_specs,
        out_specs=[pl.BlockSpec(s.shape, lambda i: (0, 0, 0)) for s in out_shape],
        scratch_shapes=[
            pltpu.VMEM((height, width), BF16),
            pltpu.VMEM((2, height, LANES), F32),
            pltpu.VMEM((height, width), F32),
        ],
        compiler_params=pltpu.CompilerParams(vmem_limit_bytes=VMEM_LIMIT),
        cost_estimate=pl.CostEstimate(
            flops=6 * work * width * hidden,
            bytes_accessed=6 * width * hidden * (2 if spare_rows else 1) + 4 * height * width,
            transcendentals=work * hidden,
        ),
        name=name,
    )(*operands)


def add(a, b):
    return (a.astype(F32) + b.astype(F32)).astype(BF16)


def per_device(
    tokens,
    route_ids,
    route_weights,
    modulation,
    partner,
    w_gate,
    w_up,
    w_down,
    spare_gate,
    spare_up,
    spare_down,
):
    experts = lax.axis_size("expert")
    shards = lax.axis_size("tensor")
    rows, width = tokens.shape
    capacity = 2 * rows // experts
    columns = width // shards
    chips = experts // 2
    shard = lax.axis_index("tensor")
    home_set = (w_gate, w_up, w_down)
    spare_set = (spare_gate, spare_up, spare_down)

    def core_swap(a):
        return lax.ppermute(a, "expert", [(e, e ^ 1) for e in range(experts)])

    def chip_hop(a, k):
        return lax.ppermute(a, "expert", [(e, (e + 2 * k) % experts) for e in range(experts)])

    def reduce_tensor(a):
        distance = 1
        while distance < shards:
            pairs = a.reshape((a.shape[0] // 2, 2) + a.shape[1:])
            bit = (shard // distance) % 2
            keep = lax.dynamic_index_in_dim(pairs, bit, 1, keepdims=False)
            give = lax.dynamic_index_in_dim(pairs, 1 - bit, 1, keepdims=False)
            got = lax.ppermute(give, "tensor", [(t, t ^ distance) for t in range(shards)])
            a = add(keep, got)
            distance *= 2
        return a[0]

    def deliver(a, k):
        got = []
        for j in range(shards):
            pairs = [
                (e * shards + t, ((e + 2 * k) % experts) * shards + (t + j) % shards)
                for e in range(experts)
                for t in range(shards)
            ]
            block = lax.dynamic_index_in_dim(a, (shard + j) % shards, 0, keepdims=False)
            got.append(lax.ppermute(block, ("expert", "tensor"), pairs))
        return got

    late, early, meta = prepare(tokens, route_ids, route_weights, modulation, experts, capacity)
    late_span = (capacity, rows - capacity)
    early_span = (0, capacity)

    hops = {}
    for k in range(1, chips):
        hops[k] = (chip_hop(meta, k), chip_hop(late, k), chip_hop(early, k))
    near = (core_swap(meta), core_swap(late), core_swap(early))
    call = functools.partial(
        ffn, partner=partner, home_set=home_set, spare_set=spare_set, experts=experts, shards=shards
    )

    late_keep, late_give, early_keep, early_give = call(
        "ffn_near",
        [late, near[1], early, near[2]],
        [meta, near[0], meta, near[0]],
        (late_span, late_span, early_span, early_span),
        2 * late_span[1],
    )
    early_sum = [reduce_tensor(add(early_keep, core_swap(early_give)))]
    late_sum = [reduce_tensor(add(late_keep, core_swap(late_give)))]

    for k in range(1, chips):
        meta_k, late_k, early_k = hops[k]
        meta_o, late_o, early_o = core_swap(meta_k), core_swap(late_k), core_swap(early_k)
        late_keep, late_give = call(
            "ffn_late", [late_k, late_o], [meta_k, meta_o], (late_span, late_span), 2 * late_span[1]
        )
        late_sum.append(chip_hop(reduce_tensor(add(late_keep, core_swap(late_give))), -k))
        early_keep, early_give = call("ffn_early", [early_k, early_o], [meta_k, meta_o], (early_span, early_span), 0)
        early_sum += deliver(add(early_keep, core_swap(early_give)), -k)

    def total(parts):
        result = parts[0].astype(F32)
        for part in parts[1:]:
            result = result + part.astype(F32)
        return result

    mixed = jnp.concatenate((total(early_sum), total(late_sum)), axis=0)
    own_cols = lax.dynamic_slice_in_dim(tokens, shard * columns, columns, 1).astype(F32)
    gate_cols = lax.dynamic_slice_in_dim(modulation[0], 2 * width + shard * columns, columns, 0)
    return (own_cols + gate_cols[None, :] * mixed).astype(BF16)


def solution(mesh):
    placed = (
        P(("groups", "expert"), None),
        P(("groups", "expert"), None),
        P(("groups", "expert"), None),
        P(("groups", "expert"), None),
        P(),
        P("expert", None, "tensor"),
        P("expert", None, "tensor"),
        P("expert", "tensor", None),
        P("expert", None, "tensor"),
        P("expert", None, "tensor"),
        P("expert", "tensor", None),
    )
    return jax.shard_map(
        per_device,
        mesh=mesh,
        in_specs=placed,
        out_specs=P(("groups", "expert"), "tensor"),
        check_vma=False,
    )
```
